32 devices in a mesh: clips: 2 (over x), tm: 8 (over z, y), cols: 2 (over core).
Axes of the slice: x: 2, y: 2, z: 4, core: 2. Of those that a mesh axis runs over, the one named last changes fastest.
Arguments:
- video: bfloat16 [64, 32, 32, 512], P(('clips', 'tm'), None, 'cols'), parts along dimension 0, may hold values from -6 to 6
- w_time: bfloat16 [3, 512, 512], replicated, may hold values from -0.15625 to 0.15625
- b_time: float32 [512], replicated, may hold values from -3 to 3
- w_down: bfloat16 [3, 512, 512], replicated, may hold values from -0.15625 to 0.15625
- b_down: float32 [512], replicated, may hold values from -3 to 3
- w_space: bfloat16 [9, 512, 512], replicated, may hold values from -0.09375 to 0.09375
- b_space: float32 [512], replicated, may hold values from -3 to 3
- gain: float32 [512], replicated, may hold values from 0.1 to 1.9
- w_query: bfloat16 [512, 512], replicated, may hold values from -30 to 30
- w_key: bfloat16 [512, 512], replicated, may hold values from -0.25 to 0.25
- w_value: bfloat16 [512, 512], replicated, may hold values from -0.25 to 0.25
- w_out: bfloat16 [512, 512], replicated, may hold values from -0.25 to 0.25
Outputs:
- encoded: bfloat16 [32, 32, 32, 512], P(('clips', 'tm'), None, 'cols'), parts along dimension 0
The draws below stay inside these ranges and needn't reach their ends.
There are 2 independent parts, one for each index of `clips`. The reference program is written for one: setup_inputs(seed, part) draws one part's arguments, and reference() takes and returns one part's arrays. A program takes and returns all parts, laid end to end along the dimension named above; an argument that names none is the same for every part. Nothing has to cross between parts.
All inputs are finite; a program needn't handle non-finite values.
Results may differ from the reference program's by a relative error of at most 0.019.
The reference program's roundings to bfloat16 on the way (of `lifted`, `reduced`, `spatial`, `normed`, `query`, `probs` and `context`) count: a program that leaves them out, or rounds other values in their place, can miss the bound.
Values may be sent and summed in bfloat16 or wider, within the bound.
A program may use at most 64 MiB of HBM per device.

```python
import jax
import jax.numpy as jnp
from jax import lax

C = 512
H = 32
W = 32
FRAMES = 32


def draw_w_query(key, part):
    values = jax.random.truncated_normal(key, -4.0, 4.0, (C, C), jnp.float32) * C ** (-0.5)
    return values.astype(jnp.bfloat16)


def block_levels(stream_key, extent, shards, smallest, high):
    def one(position, parts):
        steps = jax.random.uniform(jax.random.fold_in(jax.random.fold_in(stream_key, 6), position), (parts,), jnp.float32, smallest / len(shards), high / len(shards))
        return jnp.repeat(jnp.exp(steps), extent[position] // parts).reshape((-1,) + (1,) * (len(extent) - position - 1))

    factor_of = one(*shards[0])
    for cut in shards[1:]:
        factor_of = factor_of * one(*cut)
    return factor_of


def gaussian(key, dims, scale, most, pieces=(), kind=jnp.bfloat16):
    entries = scale * jax.random.normal(key, dims, jnp.float32)
    if pieces:
        entries = entries * block_levels(key, dims, pieces, -0.22, 0.18)
    return jnp.clip(entries, -most, most).astype(kind)


def setup_inputs(seed: int = 0, part: int = 0) -> dict:
    streams_of = jax.random.split(jax.random.key(seed), 13)
    part_keys = jax.random.split(jax.random.fold_in(streams_of[12], part), 13)
    video = gaussian(part_keys[0], (FRAMES, H, W, C), 1.0, 6.0, ((0, 8), (2, 2)))
    w_time = gaussian(streams_of[1], (3, C, C), (3 * C) ** -0.5, 0.15625)
    b_time = gaussian(streams_of[2], (C,), 0.5, 3.0, (), jnp.float32)
    w_down = gaussian(streams_of[3], (3, C, C), (3 * C) ** -0.5, 0.15625)
    b_down = gaussian(streams_of[4], (C,), 0.5, 3.0, (), jnp.float32)
    w_space = gaussian(streams_of[5], (9, C, C), (9 * C) ** -0.5, 0.09375)
    b_space = gaussian(streams_of[6], (C,), 0.5, 3.0, (), jnp.float32)
    gain = jnp.clip(1.0 + 0.18 * jax.random.normal(streams_of[7], (C,), jnp.float32), 0.1, 1.9)
    w_query = draw_w_query(jax.random.fold_in(streams_of[12], 71), part)
    w_key = gaussian(streams_of[9], (C, C), C ** -0.5, 0.25)
    w_value = gaussian(streams_of[10], (C, C), C ** -0.5, 0.25)
    w_out = gaussian(streams_of[11], (C, C), C ** -0.5, 0.25)
    return {"video": video, "w_time": w_time, "b_time": b_time, "w_down": w_down, "b_down": b_down, "w_space": w_space, "b_space": b_space, "gain": gain, "w_query": w_query, "w_key": w_key, "w_value": w_value, "w_out": w_out}


epsilon = 1e-06

def attend(sequence, gain, w_query, w_key, w_value, w_out):
    frames, pixels, channels = sequence.shape
    wide = sequence.astype(jnp.float32)
    scale = lax.rsqrt(lax.optimization_barrier(jnp.mean(wide * wide, axis=-1, keepdims=True)) + epsilon)
    normed = (wide * scale * gain).astype(jnp.bfloat16).reshape(-1, channels)
    query = jnp.dot(normed, w_query, preferred_element_type=jnp.float32).astype(jnp.bfloat16).reshape(frames, pixels, channels)
    key = jnp.dot(normed, w_key, preferred_element_type=jnp.float32).astype(jnp.bfloat16).reshape(frames, pixels, channels)
    value = jnp.dot(normed, w_value, preferred_element_type=jnp.float32).astype(jnp.bfloat16).reshape(frames, pixels, channels)
    scores = jnp.einsum('spc,tpc->pst', query.astype(jnp.float32), key.astype(jnp.float32)) * channels ** (-0.5)
    steps = jnp.arange(frames)
    allowed = steps[None, :] <= steps[:, None]
    scores = jnp.where(allowed[None], scores, -1e+30)
    largest = lax.optimization_barrier(jnp.max(scores, axis=-1, keepdims=True))
    probs = jnp.exp(scores - largest)
    probs = probs / lax.optimization_barrier(jnp.sum(probs, axis=-1, keepdims=True))
    probs = probs.astype(jnp.bfloat16)
    context = jnp.einsum('pst,tpc->spc', probs.astype(jnp.float32), value.astype(jnp.float32)).astype(jnp.bfloat16)
    mixed = jnp.dot(context.reshape(-1, channels), w_out, preferred_element_type=jnp.float32).reshape(frames, pixels, channels)
    return (wide + mixed).astype(jnp.bfloat16)

def reference(video, w_time, b_time, w_down, b_down, w_space, b_space, gain, w_query, w_key, w_value, w_out):
    frames, height, columns, channels = video.shape
    shape = (frames, height, columns, channels)
    padded = jnp.concatenate([jnp.zeros((2, height, columns, channels), video.dtype), video], 0)
    summed = jnp.zeros((frames * height * columns, channels), jnp.float32) + b_time
    for offset in range(3):
        summed = summed + jnp.dot(padded[2 - offset:2 - offset + frames].reshape(-1, channels), w_time[offset], preferred_element_type=jnp.float32)
    lifted = (video.astype(jnp.float32) + jax.nn.silu(summed.reshape(shape))).astype(jnp.bfloat16)
    shifted = jnp.concatenate([jnp.zeros((1, height, columns, channels), lifted.dtype), lifted], 0)
    halves = frames // 2
    taps = [shifted[2:frames + 1:2], shifted[1:frames:2], shifted[0:frames - 1:2]]
    summed = jnp.zeros((halves * height * columns, channels), jnp.float32) + b_down
    for offset in range(3):
        summed = summed + jnp.dot(taps[offset].reshape(-1, channels), w_down[offset], preferred_element_type=jnp.float32)
    reduced = summed.reshape(halves, height, columns, channels).astype(jnp.bfloat16)
    framed = jnp.pad(reduced, ((0, 0), (1, 1), (1, 1), (0, 0)))
    summed = jnp.zeros((halves * height * columns, channels), jnp.float32) + b_space
    for row_tap in range(3):
        for col_tap in range(3):
            window = framed[:, row_tap:row_tap + height, col_tap:col_tap + columns]
            summed = summed + jnp.dot(window.reshape(-1, channels), w_space[3 * row_tap + col_tap], preferred_element_type=jnp.float32)
    spatial = (reduced.astype(jnp.float32) + jax.nn.silu(summed.reshape(halves, height, columns, channels))).astype(jnp.bfloat16)
    encoded = attend(spatial.reshape(halves, height * columns, channels), gain, w_query, w_key, w_value, w_out)
    return encoded.reshape(halves, height, columns, channels)
```

```python
from functools import partial

import jax
import jax.numpy as jnp
from jax import lax
from jax.experimental import pallas as pl
from jax.experimental.pallas import tpu as pltpu
from jax.sharding import PartitionSpec as P

epsilon = 1e-06
MESH = pl.DeviceIdType.MESH


def passed_along(value, axis, steps):
    count = lax.axis_size(axis)
    first, last = (max(0, -steps), min(count, count - steps))
    return lax.ppermute(value, axis, [(source, source + steps) for source in range(first, last)])


def padded(x, sides, width):
    for axis, dim in sides:
        devices, length = (lax.axis_size(axis), x.shape[dim])
        up = [(i, (i + 1) % devices) for i in range(devices - 1)]
        down = [(j, i) for i, j in up]
        last = lax.slice_in_dim(x, length - width, length, axis=dim)
        first = lax.slice_in_dim(x, 0, width, axis=dim)
        before = lax.ppermute(last, axis, up)
        after = lax.ppermute(first, axis, down)
        x = jnp.concatenate([before, x, after], axis=dim)
    return x


def attention_kernel(
    x_ref, gain_ref, wq_ref, wk_ref, wv_ref, wo_ref, y_ref,
    held, done, send_sem, recv_sem, back_sem, home_sem,
):
    halves, owners, chunks, pixels, channels = x_ref.shape
    frames = owners * halves
    rows = frames * pixels
    me = lax.axis_index("tm")

    barrier = pltpu.get_barrier_semaphore()

    def greet(k, _):
        peer = lax.rem(me + k, owners)
        pl.semaphore_signal(barrier, inc=1, device_id={"tm": peer}, device_id_type=MESH)
        return 0

    lax.fori_loop(1, owners, greet, 0)
    pl.semaphore_wait(barrier, owners - 1)

    def outward(c, peer, slot, source):
        return pltpu.make_async_remote_copy(
            src_ref=x_ref.at[:, peer, c],
            dst_ref=held.at[c, source],
            send_sem=send_sem.at[c, slot],
            recv_sem=recv_sem.at[c, source],
            device_id={"tm": peer},
            device_id_type=MESH,
        )

    def homeward(c, peer, slot, source):
        return pltpu.make_async_remote_copy(
            src_ref=done.at[c, peer],
            dst_ref=y_ref.at[:, source, c],
            send_sem=back_sem.at[c, slot],
            recv_sem=home_sem.at[c, source],
            device_id={"tm": peer},
            device_id_type=MESH,
        )

    for c in range(chunks):
        def send(k, _):
            outward(c, lax.rem(me + k, owners), k, me).start()
            return 0

        lax.fori_loop(1, owners, send, 0)

    place = lax.broadcasted_iota(jnp.int32, (rows, rows), 0)
    other = lax.broadcasted_iota(jnp.int32, (rows, rows), 1)
    allowed = (lax.rem(place, pixels) == lax.rem(other, pixels)) & (other <= place)

    for c in range(chunks):
        held[c, me] = x_ref[:, me, c]

        def arrive(k, _):
            source = lax.rem(me + owners - k, owners)
            outward(c, lax.rem(me + k, owners), k, source).wait_recv()
            return 0

        lax.fori_loop(1, owners, arrive, 0)
        wide = held[c].reshape(rows, channels).astype(jnp.float32)
        scale = lax.rsqrt(jnp.mean(wide * wide, axis=-1, keepdims=True) + epsilon)
        normed = (wide * scale * gain_ref[...]).astype(jnp.bfloat16)
        query = jnp.dot(normed, wq_ref[...], preferred_element_type=jnp.float32).astype(jnp.bfloat16)
        key = jnp.dot(normed, wk_ref[...], preferred_element_type=jnp.float32).astype(jnp.bfloat16)
        value = jnp.dot(normed, wv_ref[...], preferred_element_type=jnp.float32).astype(jnp.bfloat16)
        scores = lax.dot_general(
            query, key, (((1,), (1,)), ((), ())), preferred_element_type=jnp.float32
        ) * channels ** (-0.5)
        scores = jnp.where(allowed, scores, -1e30)
        largest = jnp.max(scores, axis=-1, keepdims=True)
        probs = jnp.exp(scores - largest)
        probs = (probs / jnp.sum(probs, axis=-1, keepdims=True)).astype(jnp.bfloat16)
        context = jnp.dot(probs, value, preferred_element_type=jnp.float32).astype(jnp.bfloat16)
        mixed = jnp.dot(context, wo_ref[...], preferred_element_type=jnp.float32)
        result = (wide + mixed).astype(jnp.bfloat16)
        done[c] = result.reshape(owners, halves, pixels, channels)

        def back(k, _):
            homeward(c, lax.rem(me + k, owners), k, me).start()
            return 0

        lax.fori_loop(1, owners, back, 0)
        y_ref[:, me, c] = done[c, me]

    for c in range(chunks):
        def finish(k, _):
            peer, source = lax.rem(me + k, owners), lax.rem(me + owners - k, owners)
            outward(c, peer, k, me).wait_send()
            homeward(c, peer, k, me).wait_send()
            homeward(c, peer, k, source).wait_recv()
            return 0

        lax.fori_loop(1, owners, finish, 0)


def attend(spatial, gain, w_query, w_key, w_value, w_out):
    halves, height, strip, channels = spatial.shape
    owners = lax.axis_size("tm")
    owned = height * strip // owners
    pixels = min(16, owned)
    chunks = owned // pixels
    vmem = pl.BlockSpec(memory_space=pltpu.VMEM)
    result = pl.pallas_call(
        attention_kernel,
        out_shape=jax.ShapeDtypeStruct((halves, owners, chunks, pixels, channels), jnp.bfloat16),
        in_specs=[vmem] * 6,
        out_specs=vmem,
        scratch_shapes=[
            pltpu.VMEM((chunks, owners, halves, pixels, channels), jnp.bfloat16),
            pltpu.VMEM((chunks, owners, halves, pixels, channels), jnp.bfloat16),
            pltpu.SemaphoreType.DMA((chunks, owners)),
            pltpu.SemaphoreType.DMA((chunks, owners)),
            pltpu.SemaphoreType.DMA((chunks, owners)),
            pltpu.SemaphoreType.DMA((chunks, owners)),
        ],
        compiler_params=pltpu.CompilerParams(
            collective_id=0, has_side_effects=True, vmem_limit_bytes=48 * 1024 * 1024
        ),
    )(
        spatial.reshape(halves, owners, chunks, pixels, channels),
        gain.reshape(1, channels), w_query, w_key, w_value, w_out,
    )
    return result.reshape(halves, height, strip, channels)


def temporal(extended, weights, bias, first, count):
    _, height, strip, channels = extended.shape
    summed = jnp.zeros((count * height * strip, channels), jnp.float32) + bias
    for offset in range(3):
        window = extended[first - offset : first - offset + count]
        summed = summed + jnp.dot(
            window.reshape(-1, channels), weights[offset], preferred_element_type=jnp.float32
        )
    return summed.reshape(count, height, strip, channels)


def lift(extended, weights, bias, first, count):
    summed = temporal(extended, weights, bias, first, count)
    return (extended[first : first + count].astype(jnp.float32) + jax.nn.silu(summed)).astype(jnp.bfloat16)


def per_device(
    video, w_time, b_time, w_down, b_down, w_space, b_space, gain, w_query, w_key, w_value, w_out
):
    frames, height, strip, channels = video.shape
    late = lift(video, w_time, b_time, 2, frames - 2)
    before = passed_along(video[frames - 2 :], "tm", 1)
    carried = passed_along(late[-1:], "tm", 1)
    extended = jnp.concatenate([before, video[:2]], 0)
    early = lift(extended, w_time, b_time, 2, 2)
    lifted_ext = jnp.concatenate([carried, early, late], 0)
    halves = frames // 2
    taps = [lifted_ext[2 : frames + 1 : 2], lifted_ext[1:frames:2], lifted_ext[0 : frames - 1 : 2]]
    summed = jnp.zeros((halves * height * strip, channels), jnp.float32) + b_down
    for offset in range(3):
        summed = summed + jnp.dot(
            taps[offset].reshape(-1, channels), w_down[offset], preferred_element_type=jnp.float32
        )
    reduced = summed.reshape(halves, height, strip, channels).astype(jnp.bfloat16)
    framed = padded(reduced, (("cols", 2),), 1)
    framed = jnp.pad(framed, ((0, 0), (1, 1), (0, 0), (0, 0)))
    summed = jnp.zeros((halves * height * strip, channels), jnp.float32) + b_space
    for row_tap in range(3):
        for col_tap in range(3):
            window = framed[:, row_tap : row_tap + height, col_tap : col_tap + strip]
            summed = summed + jnp.dot(
                window.reshape(-1, channels),
                w_space[3 * row_tap + col_tap],
                preferred_element_type=jnp.float32,
            )
    spatial = (
        reduced.astype(jnp.float32) + jax.nn.silu(summed.reshape(halves, height, strip, channels))
    ).astype(jnp.bfloat16)
    return attend(spatial, gain, w_query, w_key, w_value, w_out)


def solution(mesh):
    return jax.shard_map(
        per_device,
        mesh=mesh,
        in_specs=(P(("clips", "tm"), None, "cols", None),) + (P(),) * 11,
        out_specs=P(("clips", "tm"), None, "cols", None),
        check_vma=False,
    )
```

```python
from functools import partial

import jax
import jax.numpy as jnp
from jax import lax
from jax.experimental import pallas as pl
from jax.experimental.pallas import tpu as pltpu
from jax.sharding import PartitionSpec as P

epsilon = 1e-06
MESH = pl.DeviceIdType.MESH


def block_kernel(
    shape, video, wt_hbm, bt, wd_hbm, bd, ws_hbm, bs, gain, wq_hbm, wk_hbm, wv_hbm, wo_hbm, y_ref,
    wt, wd, ws, wq, wk, wv, wo, before, carried, lifted, left_of, middle, right_of, partial_sum,
    edges, halo, spatial, held, done,
    load_sem, frame_send, frame_recv, edge_send, edge_recv, send_sem, recv_sem, back_sem, home_sem,
):
    height, strip = shape
    frames, area, channels = video.shape
    halves, owners, chunks, pixels, _ = y_ref.shape
    total = owners * halves
    rows = total * pixels
    me, col, cols = lax.axis_index("tm"), lax.axis_index("cols"), lax.axis_size("cols")
    f32, bf16 = jnp.float32, jnp.bfloat16
    tile = min(256, area)
    lines = tile // strip

    loads = [
        pltpu.make_async_copy(source, target, load_sem.at[i])
        for i, (source, target) in enumerate(
            ((wt_hbm, wt), (wd_hbm, wd), (ws_hbm, ws), (wq_hbm, wq), (wk_hbm, wk), (wv_hbm, wv), (wo_hbm, wo))
        )
    ]
    for load in loads:
        load.start()

    barrier = pltpu.get_barrier_semaphore()

    def greet(k, _):
        peer = lax.rem(me + k, owners)
        pl.semaphore_signal(barrier, inc=1, device_id={"tm": peer}, device_id_type=MESH)
        return 0

    lax.fori_loop(1, owners, greet, 0)

    def greet_side(k, _):
        peer = lax.rem(col + k, cols)
        pl.semaphore_signal(barrier, inc=1, device_id={"cols": peer}, device_id_type=MESH)
        return 0

    lax.fori_loop(1, cols, greet_side, 0)
    pl.semaphore_wait(barrier, owners + cols - 2)

    def onward(i):
        source, target = (
            (video.at[frames - 1], before.at[1]),
            (video.at[frames - 2], before.at[0]),
            (lifted.at[frames - 1], carried),
        )[i]
        return pltpu.make_async_remote_copy(
            src_ref=source, dst_ref=target, send_sem=frame_send.at[i], recv_sem=frame_recv.at[i],
            device_id={"tm": lax.rem(me + 1, owners)}, device_id_type=MESH,
        )

    has_next, has_before = me < owners - 1, me > 0

    def send_on(i):
        @pl.when(has_next)
        def _():
            onward(i).start()

    def take(i):
        target = (before.at[1], before.at[0], carried)[i]

        @pl.when(has_before)
        def _():
            onward(i).wait_recv()

        @pl.when(jnp.logical_not(has_before))
        def _():
            target[...] = jnp.zeros((area, channels), bf16)

    send_on(0)
    send_on(1)

    def frame_of(f):
        return video.at[f] if f >= 0 else before.at[f + 2]

    def lift(f):
        @pl.loop(0, area // tile)
        def _(t):
            part = pl.ds(pl.multiple_of(t * tile, tile), tile)
            summed = bt[...] + jnp.dot(frame_of(f)[part], wt[0], preferred_element_type=f32)
            summed = summed + jnp.dot(frame_of(f - 1)[part], wt[1], preferred_element_type=f32)
            summed = summed + jnp.dot(frame_of(f - 2)[part], wt[2], preferred_element_type=f32)
            lifted[f, part] = (video[f, part].astype(f32) + jax.nn.silu(summed)).astype(bf16)

    def sideways(s, side):
        peer = lax.rem(col + 1, cols) if side == 0 else lax.rem(col + cols - 1, cols)
        return pltpu.make_async_remote_copy(
            src_ref=edges.at[s, side], dst_ref=halo.at[s, side],
            send_sem=edge_send.at[s, side], recv_sem=edge_recv.at[s, side],
            device_id={"cols": peer}, device_id_type=MESH,
        )

    sends_side = (col < cols - 1, col > 0)
    takes_side = (col > 0, col < cols - 1)

    def reduce_frame(s):
        top = 2 * s + 1

        @pl.loop(0, area // tile)
        def _(t):
            part = pl.ds(pl.multiple_of(t * tile, tile), tile)
            oldest = carried[part] if s == 0 else lifted[top - 2, part]
            summed = bd[...] + jnp.dot(lifted[top, part], wd[0], preferred_element_type=f32)
            summed = summed + jnp.dot(lifted[top - 1, part], wd[1], preferred_element_type=f32)
            summed = summed + jnp.dot(oldest, wd[2], preferred_element_type=f32)
            reduced = summed.astype(bf16)
            middle[s, pl.ds(1 + t * lines, lines)] = reduced.reshape(lines, strip, channels)
            wide = reduced.astype(f32).reshape(lines, strip, channels)
            line = pl.ds(pl.multiple_of(t * lines, lines), lines)
            edges[s, 0, line] = wide[:, strip - 1].astype(bf16)
            edges[s, 1, line] = wide[:, 0].astype(bf16)

        for side in range(2):
            @pl.when(sends_side[side])
            def _():
                sideways(s, side).start()

    def convolve(s):
        for shifted in (left_of, middle, right_of):
            shifted[s, 0] = jnp.zeros((strip, channels), bf16)
            shifted[s, height + 1] = jnp.zeros((strip, channels), bf16)

        def taps(shifted, t, b, summed):
            for a in range(3):
                window = shifted[s, pl.ds(t * lines + a, lines)].reshape(tile, channels)
                summed = summed + jnp.dot(window, ws[3 * a + b], preferred_element_type=f32)
            return summed

        @pl.loop(0, area // tile)
        def _(t):
            part = pl.ds(pl.multiple_of(t * tile, tile), tile)
            partial_sum[part] = taps(middle, t, 1, jnp.zeros((tile, channels), f32) + bs[...])

        for side in range(2):
            @pl.when(takes_side[side])
            def _():
                sideways(s, side).wait_recv()

            @pl.when(jnp.logical_not(takes_side[side]))
            def _():
                halo[s, side] = jnp.zeros((height, channels), bf16)

        @pl.loop(0, area // tile)
        def _(t):
            line = pl.ds(pl.multiple_of(t * lines, lines), lines)
            wide = middle[s, pl.ds(1 + t * lines, lines)].astype(f32).reshape(tile, channels)
            place = lax.rem(lax.broadcasted_iota(jnp.int32, (tile, channels), 0), strip)

            def spread(side):
                column = halo[s, side, line].astype(f32)
                return jnp.broadcast_to(column[:, None, :], (lines, strip, channels)).reshape(tile, channels)

            lower = jnp.where(place == 0, spread(0), pltpu.roll(wide, 1, 0))
            upper = jnp.where(place == strip - 1, spread(1), pltpu.roll(wide, tile - 1, 0))
            left_of[s, pl.ds(1 + t * lines, lines)] = lower.astype(bf16).reshape(lines, strip, channels)
            right_of[s, pl.ds(1 + t * lines, lines)] = upper.astype(bf16).reshape(lines, strip, channels)

        groups = tile // pixels

        @pl.loop(0, area // tile)
        def _(t):
            part = pl.ds(pl.multiple_of(t * tile, tile), tile)
            summed = taps(left_of, t, 0, partial_sum[part])
            summed = taps(right_of, t, 2, summed)
            wide = middle[s, pl.ds(1 + t * lines, lines)].astype(f32).reshape(tile, channels)
            result = (wide + jax.nn.silu(summed)).astype(bf16)
            spatial[s, pl.ds(t * groups, groups)] = result.reshape(groups, pixels, channels)

    def outward(s, c, peer, slot, source):
        return pltpu.make_async_remote_copy(
            src_ref=spatial.at[s, peer * chunks + c],
            dst_ref=held.at[c, source, s],
            send_sem=send_sem.at[s, c, slot],
            recv_sem=recv_sem.at[s, c, source],
            device_id={"tm": peer},
            device_id_type=MESH,
        )

    def homeward(c, peer, slot, source):
        return pltpu.make_async_remote_copy(
            src_ref=done.at[c, peer],
            dst_ref=y_ref.at[:, source, c],
            send_sem=back_sem.at[c, slot],
            recv_sem=home_sem.at[c, source],
            device_id={"tm": peer},
            device_id_type=MESH,
        )

    def scatter(s):
        for c in range(chunks):
            def send(k, _):
                outward(s, c, lax.rem(me + k, owners), k, me).start()
                return 0

            lax.fori_loop(1, owners, send, 0)

    loads[0].wait()
    for f in range(frames - 1, 1, -1):
        lift(f)
        if f == frames - 1:
            send_on(2)
    loads[1].wait()
    for s in range(halves - 1, 1, -1):
        reduce_frame(s)
    take(0)
    lift(1)
    reduce_frame(1)
    loads[2].wait()
    for s in range(halves - 1, 0, -1):
        convolve(s)
        scatter(s)
    take(1)
    lift(0)
    take(2)
    reduce_frame(0)
    convolve(0)
    scatter(0)
    for load in loads[3:]:
        load.wait()

    place = lax.broadcasted_iota(jnp.int32, (rows, rows), 0)
    other = lax.broadcasted_iota(jnp.int32, (rows, rows), 1)
    allowed = (lax.rem(place, pixels) == lax.rem(other, pixels)) & (other <= place)

    for c in range(chunks):
        for s in range(halves):
            held[c, me, s] = spatial[s, me * chunks + c]

        def arrive(k, _):
            source = lax.rem(me + owners - k, owners)
            for s in range(halves):
                outward(s, c, lax.rem(me + k, owners), k, source).wait_recv()
            return 0

        lax.fori_loop(1, owners, arrive, 0)
        wide = held[c].reshape(rows, channels).astype(f32)
        scale = lax.rsqrt(jnp.mean(wide * wide, axis=-1, keepdims=True) + epsilon)
        normed = (wide * scale * gain[...]).astype(bf16)
        query = jnp.dot(normed, wq[...], preferred_element_type=f32).astype(bf16)
        key = jnp.dot(normed, wk[...], preferred_element_type=f32).astype(bf16)
        value = jnp.dot(normed, wv[...], preferred_element_type=f32).astype(bf16)
        scores = lax.dot_general(
            query, key, (((1,), (1,)), ((), ())), preferred_element_type=f32
        ) * channels ** (-0.5)
        scores = jnp.where(allowed, scores, -1e30)
        largest = jnp.max(scores, axis=-1, keepdims=True)
        probs = jnp.exp(scores - largest)
        probs = (probs / jnp.sum(probs, axis=-1, keepdims=True)).astype(bf16)
        context = jnp.dot(probs, value, preferred_element_type=f32).astype(bf16)
        mixed = jnp.dot(context, wo[...], preferred_element_type=f32)
        result = (wide + mixed).astype(bf16)
        done[c] = result.reshape(owners, halves, pixels, channels)

        def back(k, _):
            homeward(c, lax.rem(me + k, owners), k, me).start()
            return 0

        lax.fori_loop(1, owners, back, 0)
        y_ref[:, me, c] = done[c, me]

    @pl.when(has_next)
    def _():
        for i in range(3):
            onward(i).wait_send()

    for s in range(halves):
        for side in range(2):
            @pl.when(sends_side[side])
            def _():
                sideways(s, side).wait_send()

    for c in range(chunks):
        def finish(k, _):
            peer, source = lax.rem(me + k, owners), lax.rem(me + owners - k, owners)
            for s in range(halves):
                outward(s, c, peer, k, me).wait_send()
            homeward(c, peer, k, me).wait_send()
            homeward(c, peer, k, source).wait_recv()
            return 0

        lax.fori_loop(1, owners, finish, 0)


def per_device(
    video, w_time, b_time, w_down, b_down, w_space, b_space, gain, w_query, w_key, w_value, w_out
):
    frames, height, strip, channels = video.shape
    halves, owners, area = frames // 2, lax.axis_size("tm"), height * strip
    owned = area // owners
    pixels = min(16, owned)
    chunks = owned // pixels
    vmem = pl.BlockSpec(memory_space=pltpu.VMEM)
    hbm = pl.BlockSpec(memory_space=pl.ANY)
    bf16 = jnp.bfloat16
    square = (channels, channels)
    shifted = pltpu.VMEM((halves, height + 2, strip, channels), bf16)
    flat = lambda v: v.reshape(1, channels)
    sems = pltpu.SemaphoreType.DMA
    result = pl.pallas_call(
        partial(block_kernel, (height, strip)),
        out_shape=jax.ShapeDtypeStruct((halves, owners, chunks, pixels, channels), bf16),
        in_specs=[vmem, hbm, vmem, hbm, vmem, hbm, vmem, vmem, hbm, hbm, hbm, hbm],
        out_specs=vmem,
        scratch_shapes=[
            pltpu.VMEM((3,) + square, bf16),
            pltpu.VMEM((3,) + square, bf16),
            pltpu.VMEM((9,) + square, bf16),
            pltpu.VMEM(square, bf16),
            pltpu.VMEM(square, bf16),
            pltpu.VMEM(square, bf16),
            pltpu.VMEM(square, bf16),
            pltpu.VMEM((2, area, channels), bf16),
            pltpu.VMEM((area, channels), bf16),
            pltpu.VMEM((frames, area, channels), bf16),
            shifted,
            shifted,
            shifted,
            pltpu.VMEM((area, channels), jnp.float32),
            pltpu.VMEM((halves, 2, height, channels), bf16),
            pltpu.VMEM((halves, 2, height, channels), bf16),
            pltpu.VMEM((halves, area // pixels, pixels, channels), bf16),
            pltpu.VMEM((chunks, owners, halves, pixels, channels), bf16),
            pltpu.VMEM((chunks, owners, halves, pixels, channels), bf16),
            sems((7,)),
            sems((3,)),
            sems((3,)),
            sems((halves, 2)),
            sems((halves, 2)),
            sems((halves, chunks, owners)),
            sems((halves, chunks, owners)),
            sems((chunks, owners)),
            sems((chunks, owners)),
        ],
        compiler_params=pltpu.CompilerParams(
            collective_id=0, has_side_effects=True, vmem_limit_bytes=56 * 1024 * 1024
        ),
    )(
        video.reshape(frames, area, channels), w_time, flat(b_time), w_down, flat(b_down),
        w_space, flat(b_space), flat(gain), w_query, w_key, w_value, w_out,
    )
    return result.reshape(halves, height, strip, channels)


def solution(mesh):
    return jax.shard_map(
        per_device,
        mesh=mesh,
        in_specs=(P(("clips", "tm"), None, "cols", None),) + (P(),) * 11,
        out_specs=P(("clips", "tm"), None, "cols", None),
        check_vma=False,
    )
```

```python
from functools import partial

import jax
import jax.numpy as jnp
from jax import lax
from jax.experimental import pallas as pl
from jax.experimental.pallas import tpu as pltpu
from jax.sharding import PartitionSpec as P

epsilon = 1e-06
MESH = pl.DeviceIdType.MESH


def block_kernel(
    shape, video_hbm, wt_hbm, bt, wd_hbm, bd, ws_hbm, bs, gain, wq_hbm, wk_hbm, wv_hbm, wo_hbm, y_ref,
    wt, wd, ws, wq, wk, wv, wo, video, lifted, left_of, middle, right_of,
    edges, halo, spatial, held, done,
    load_sem, frame_send, frame_recv, edge_send, edge_recv, send_sem, recv_sem, back_sem, home_sem,
):
    height, strip = shape
    frames, area, channels = video_hbm.shape
    halves, chunks, owners, pixels, _ = y_ref.shape
    total = owners * halves
    rows = total * pixels
    me, col, cols = lax.axis_index("tm"), lax.axis_index("cols"), lax.axis_size("cols")
    f32, bf16 = jnp.float32, jnp.bfloat16
    tile = owners * pixels
    lines = tile // strip

    loads = [
        pltpu.make_async_copy(source, target, load_sem.at[i])
        for i, (source, target) in enumerate(
            (
                (video_hbm, video.at[pl.ds(2, frames)]), (wt_hbm, wt), (wd_hbm, wd), (ws_hbm, ws),
                (wq_hbm, wq), (wk_hbm, wk), (wv_hbm, wv), (wo_hbm, wo),
            )
        )
    ]
    for load in loads:
        load.start()

    barrier = pltpu.get_barrier_semaphore()

    def greet(k, _):
        peer = lax.rem(me + k, owners)
        pl.semaphore_signal(barrier, inc=1, device_id={"tm": peer}, device_id_type=MESH)
        return 0

    lax.fori_loop(1, owners, greet, 0)

    def greet_side(k, _):
        peer = lax.rem(col + k, cols)
        pl.semaphore_signal(barrier, inc=1, device_id={"cols": peer}, device_id_type=MESH)
        return 0

    lax.fori_loop(1, cols, greet_side, 0)
    pl.semaphore_wait(barrier, owners + cols - 2)

    has_next, has_before = me < owners - 1, me > 0

    def span(b):
        return pl.ds(b * tile, tile)

    def landing(i, b):
        return (video.at[1, span(b)], video.at[0, span(b)], lifted.at[0, span(b)])[i]

    def onward(i, b):
        source = (video.at[frames + 1, span(b)], video.at[frames, span(b)], lifted.at[frames, span(b)])[i]
        return pltpu.make_async_remote_copy(
            src_ref=source, dst_ref=landing(i, b),
            send_sem=frame_send.at[i, b], recv_sem=frame_recv.at[i, b],
            device_id={"tm": lax.rem(me + 1, owners)}, device_id_type=MESH,
        )

    def send_on(i, b):
        @pl.when(has_next)
        def _():
            onward(i, b).start()

    def take(i, b):
        @pl.when(has_before)
        def _():
            onward(i, b).wait_recv()

        @pl.when(jnp.logical_not(has_before))
        def _():
            landing(i, b)[...] = jnp.zeros((tile, channels), bf16)

    def stacked(ref, which, b):
        return jnp.concatenate([ref[f, span(b)] for f in which], 0)

    def lift(first, count, b):
        own = [f + 2 for f in range(first, first + count)]
        summed = jnp.dot(stacked(video, own, b), wt[0], preferred_element_type=f32)
        for k in (1, 2):
            summed = summed + jnp.dot(
                stacked(video, [f - k for f in own], b), wt[k], preferred_element_type=f32
            )
        summed = summed + bt[...]
        result = (stacked(video, own, b).astype(f32) + jax.nn.silu(summed)).astype(bf16)
        for i in range(count):
            lifted[first + 1 + i, span(b)] = result[i * tile : (i + 1) * tile]

    def sideways(b, side):
        peer = lax.rem(col + 1, cols) if side == 0 else lax.rem(col + cols - 1, cols)
        return pltpu.make_async_remote_copy(
            src_ref=edges.at[b, side], dst_ref=halo.at[b, side],
            send_sem=edge_send.at[b, side], recv_sem=edge_recv.at[b, side],
            device_id={"cols": peer}, device_id_type=MESH,
        )

    sends_side = (col < cols - 1, col > 0)
    takes_side = (col > 0, col < cols - 1)

    def window(ref, b, a):
        start = b * lines + a
        return ref[:, start : start + lines].reshape(halves * tile, channels)

    def place_band(ref, b, value):
        ref[:, 1 + b * lines : 1 + (b + 1) * lines] = value.reshape(halves, lines, strip, channels)

    def reduce_band(b):
        summed = jnp.zeros((halves * tile, channels), f32) + bd[...]
        for k in range(3):
            which = [2 * s + 2 - k for s in range(halves)]
            summed = summed + jnp.dot(stacked(lifted, which, b), wd[k], preferred_element_type=f32)
        reduced = summed.astype(bf16)
        place_band(middle, b, reduced)
        wide = reduced.astype(f32).reshape(halves, lines, strip, channels)
        edges[b, 0] = wide[:, :, strip - 1].astype(bf16)
        edges[b, 1] = wide[:, :, 0].astype(bf16)
        for side in range(2):
            @pl.when(sends_side[side])
            def _():
                sideways(b, side).start()

    def shift_band(b):
        for side in range(2):
            @pl.when(takes_side[side])
            def _():
                sideways(b, side).wait_recv()

            @pl.when(jnp.logical_not(takes_side[side]))
            def _():
                halo[b, side] = jnp.zeros((halves, lines, channels), bf16)

        size = halves * tile
        wide = window(middle, b, 1).astype(f32)
        place = lax.rem(lax.broadcasted_iota(jnp.int32, (size, channels), 0), strip)

        def spread(side):
            column = halo[b, side].astype(f32)
            column = jnp.broadcast_to(column[:, :, None, :], (halves, lines, strip, channels))
            return column.reshape(size, channels)

        lower = jnp.where(place == 0, spread(0), pltpu.roll(wide, 1, 0))
        upper = jnp.where(place == strip - 1, spread(1), pltpu.roll(wide, size - 1, 0))
        place_band(left_of, b, lower.astype(bf16))
        place_band(right_of, b, upper.astype(bf16))

    def convolve_band(b):
        summed = jnp.zeros((halves * tile, channels), f32) + bs[...]
        for k, shifted in ((1, middle), (0, left_of), (2, right_of)):
            for a in range(3):
                summed = summed + jnp.dot(
                    window(shifted, b, a), ws[3 * a + k], preferred_element_type=f32
                )
        result = (window(middle, b, 1).astype(f32) + jax.nn.silu(summed)).astype(bf16)
        spatial[b] = result.reshape(halves, owners, pixels, channels)

    def outward(c, peer, slot, source):
        return pltpu.make_async_remote_copy(
            src_ref=spatial.at[c, :, peer],
            dst_ref=held.at[c, source],
            send_sem=send_sem.at[c, slot],
            recv_sem=recv_sem.at[c, source],
            device_id={"tm": peer},
            device_id_type=MESH,
        )

    def homeward(c, peer, slot, source):
        return pltpu.make_async_remote_copy(
            src_ref=done.at[c, peer],
            dst_ref=y_ref.at[:, c, source],
            send_sem=back_sem.at[c, slot],
            recv_sem=home_sem.at[c, source],
            device_id={"tm": peer},
            device_id_type=MESH,
        )

    def scatter(c):
        def send(k, _):
            outward(c, lax.rem(me + k, owners), k, me).start()
            return 0

        lax.fori_loop(1, owners, send, 0)

    def attend(c):
        held[c, me] = spatial[c, :, me]

        def arrive(k, _):
            source = lax.rem(me + owners - k, owners)
            outward(c, lax.rem(me + k, owners), k, source).wait_recv()
            return 0

        lax.fori_loop(1, owners, arrive, 0)
        place = lax.broadcasted_iota(jnp.int32, (rows, rows), 0)
        other = lax.broadcasted_iota(jnp.int32, (rows, rows), 1)
        allowed = (lax.rem(place, pixels) == lax.rem(other, pixels)) & (other <= place)
        wide = held[c].reshape(rows, channels).astype(f32)
        scale = lax.rsqrt(jnp.mean(wide * wide, axis=-1, keepdims=True) + epsilon)
        normed = (wide * scale * gain[...]).astype(bf16)
        query = jnp.dot(normed, wq[...], preferred_element_type=f32).astype(bf16)
        key = jnp.dot(normed, wk[...], preferred_element_type=f32).astype(bf16)
        value = jnp.dot(normed, wv[...], preferred_element_type=f32).astype(bf16)
        scores = lax.dot_general(
            query, key, (((1,), (1,)), ((), ())), preferred_element_type=f32
        ) * channels ** (-0.5)
        scores = jnp.where(allowed, scores, -1e30)
        largest = jnp.max(scores, axis=-1, keepdims=True)
        probs = jnp.exp(scores - largest)
        probs = (probs / jnp.sum(probs, axis=-1, keepdims=True)).astype(bf16)
        context = jnp.dot(probs, value, preferred_element_type=f32).astype(bf16)
        mixed = jnp.dot(context, wo[...], preferred_element_type=f32)
        result = (wide + mixed).astype(bf16)
        done[c] = result.reshape(owners, halves, pixels, channels)

        def back(k, _):
            homeward(c, lax.rem(me + k, owners), k, me).start()
            return 0

        lax.fori_loop(1, owners, back, 0)
        y_ref[:, c, me] = done[c, me]

    for shifted in (left_of, middle, right_of):
        for line in (0, height + 1):
            shifted[:, line] = jnp.zeros((halves, strip, channels), bf16)
    loads[0].wait()
    send_on(0, 0)
    send_on(1, 0)
    loads[1].wait()
    for b in range(chunks):
        lift(2, frames - 2, b)
        send_on(2, b)
        if b + 1 < chunks:
            send_on(0, b + 1)
            send_on(1, b + 1)
    for load in loads[2:]:
        load.wait()
    for b in range(chunks + 1):
        if b < chunks:
            take(0, b)
            take(1, b)
            lift(0, 2, b)
            take(2, b)
            reduce_band(b)
            if b >= 2:
                attend(b - 2)
            shift_band(b)
        if b >= 1:
            convolve_band(b - 1)
            scatter(b - 1)
    for c in range(max(0, chunks - 2), chunks):
        attend(c)

    @pl.when(has_next)
    def _():
        for b in range(chunks):
            for i in range(3):
                onward(i, b).wait_send()

    for b in range(chunks):
        for side in range(2):
            @pl.when(sends_side[side])
            def _():
                sideways(b, side).wait_send()

    for c in range(chunks):
        def finish(k, _):
            peer, source = lax.rem(me + k, owners), lax.rem(me + owners - k, owners)
            outward(c, peer, k, me).wait_send()
            homeward(c, peer, k, me).wait_send()
            homeward(c, peer, k, source).wait_recv()
            return 0

        lax.fori_loop(1, owners, finish, 0)


def per_device(
    video, w_time, b_time, w_down, b_down, w_space, b_space, gain, w_query, w_key, w_value, w_out
):
    frames, height, strip, channels = video.shape
    halves, owners, area = frames // 2, lax.axis_size("tm"), height * strip
    owned = area // owners
    pixels = min(16, owned)
    chunks = owned // pixels
    vmem = pl.BlockSpec(memory_space=pltpu.VMEM)
    hbm = pl.BlockSpec(memory_space=pltpu.HBM)
    bf16 = jnp.bfloat16
    square = (channels, channels)
    shifted = pltpu.VMEM((halves, height + 2, strip, channels), bf16)
    flat = lambda v: v.reshape(1, channels)
    sems = pltpu.SemaphoreType.DMA
    result = pl.pallas_call(
        partial(block_kernel, (height, strip)),
        out_shape=jax.ShapeDtypeStruct((halves, chunks, owners, pixels, channels), bf16),
        in_specs=[hbm, hbm, vmem, hbm, vmem, hbm, vmem, vmem, hbm, hbm, hbm, hbm],
        out_specs=vmem,
        scratch_shapes=[
            pltpu.VMEM((3,) + square, bf16),
            pltpu.VMEM((3,) + square, bf16),
            pltpu.VMEM((9,) + square, bf16),
            pltpu.VMEM(square, bf16),
            pltpu.VMEM(square, bf16),
            pltpu.VMEM(square, bf16),
            pltpu.VMEM(square, bf16),
            pltpu.VMEM((frames + 2, area, channels), bf16),
            pltpu.VMEM((frames + 1, area, channels), bf16),
            shifted,
            shifted,
            shifted,
            pltpu.VMEM((chunks, 2, halves, height // chunks, channels), bf16),
            pltpu.VMEM((chunks, 2, halves, height // chunks, channels), bf16),
            pltpu.VMEM((chunks, halves, owners, pixels, channels), bf16),
            pltpu.VMEM((chunks, owners, halves, pixels, channels), bf16),
            pltpu.VMEM((chunks, owners, halves, pixels, channels), bf16),
            sems((8,)),
            sems((3, chunks)),
            sems((3, chunks)),
            sems((chunks, 2)),
            sems((chunks, 2)),
            sems((chunks, owners)),
            sems((chunks, owners)),
            sems((chunks, owners)),
            sems((chunks, owners)),
        ],
        compiler_params=pltpu.CompilerParams(
            collective_id=0, has_side_effects=True, vmem_limit_bytes=44 * 1024 * 1024
        ),
    )(
        video.reshape(frames, area, channels), w_time, flat(b_time), w_down, flat(b_down),
        w_space, flat(b_space), flat(gain), w_query, w_key, w_value, w_out,
    )
    return result.reshape(halves, height, strip, channels)


def solution(mesh):
    return jax.shard_map(
        per_device,
        mesh=mesh,
        in_specs=(P(("clips", "tm"), None, "cols", None),) + (P(),) * 11,
        out_specs=P(("clips", "tm"), None, "cols", None),
        check_vma=False,
    )
```

```python
from functools import partial

import jax
import jax.numpy as jnp
from jax import lax
from jax.experimental import pallas as pl
from jax.experimental.pallas import tpu as pltpu
from jax.sharding import PartitionSpec as P

epsilon = 1e-06
MESH = pl.DeviceIdType.MESH


def block_kernel(
    shape, video_hbm, wt_hbm, bt, wd_hbm, bd, ws_hbm, bs, gain, wq_hbm, wk_hbm, wv_hbm, wo_hbm, y_ref,
    wt, wd, ws, wq, wk, wv, wo, video, lifted, left_of, middle, right_of,
    edges, halo, spatial, held, done,
    load_sem, frame_send, frame_recv, edge_send, edge_recv, send_sem, recv_sem, back_sem, home_sem,
):
    height, strip = shape
    frames, area, channels = video_hbm.shape
    halves, chunks, owners, pixels, _ = y_ref.shape
    total = owners * halves
    rows = total * pixels
    me, col, cols = lax.axis_index("tm"), lax.axis_index("cols"), lax.axis_size("cols")
    f32, bf16 = jnp.float32, jnp.bfloat16
    tile = owners * pixels
    lines = tile // strip

    loads = [
        pltpu.make_async_copy(source, target, load_sem.at[i])
        for i, (source, target) in enumerate(
            (
                (video_hbm, video.at[pl.ds(2, frames)]), (wt_hbm, wt), (wd_hbm, wd), (ws_hbm, ws),
                (wq_hbm, wq), (wk_hbm, wk), (wv_hbm, wv), (wo_hbm, wo),
            )
        )
    ]
    for load in loads:
        load.start()

    barrier = pltpu.get_barrier_semaphore()

    def greet(k, _):
        peer = lax.rem(me + k, owners)
        pl.semaphore_signal(barrier, inc=1, device_id={"tm": peer}, device_id_type=MESH)
        return 0

    lax.fori_loop(1, owners, greet, 0)

    def greet_side(k, _):
        peer = lax.rem(col + k, cols)
        pl.semaphore_signal(barrier, inc=1, device_id={"cols": peer}, device_id_type=MESH)
        return 0

    lax.fori_loop(1, cols, greet_side, 0)
    pl.semaphore_wait(barrier, owners + cols - 2)

    has_next, has_before = me < owners - 1, me > 0

    def span(b):
        return pl.ds(b * tile, tile)

    def landing(i, b):
        return (video.at[1, span(b)], video.at[0, span(b)], lifted.at[0, span(b)])[i]

    def onward(i, b):
        source = (video.at[frames + 1, span(b)], video.at[frames, span(b)], lifted.at[frames, span(b)])[i]
        return pltpu.make_async_remote_copy(
            src_ref=source, dst_ref=landing(i, b),
            send_sem=frame_send.at[i, b], recv_sem=frame_recv.at[i, b],
            device_id={"tm": lax.rem(me + 1, owners)}, device_id_type=MESH,
        )

    def send_on(i, b):
        @pl.when(has_next)
        def _():
            onward(i, b).start()

    def take(i, b):
        @pl.when(has_before)
        def _():
            onward(i, b).wait_recv()

        @pl.when(jnp.logical_not(has_before))
        def _():
            landing(i, b)[...] = jnp.zeros((tile, channels), bf16)

    def stacked(ref, which, b):
        return jnp.concatenate([ref[f, span(b)] for f in which], 0)

    def lift(first, count, b):
        own = [f + 2 for f in range(first, first + count)]
        summed = jnp.dot(stacked(video, own, b), wt[0], preferred_element_type=f32)
        for k in (1, 2):
            summed = summed + jnp.dot(
                stacked(video, [f - k for f in own], b), wt[k], preferred_element_type=f32
            )
        summed = summed + bt[...]
        result = (stacked(video, own, b).astype(f32) + jax.nn.silu(summed)).astype(bf16)
        for i in range(count):
            lifted[first + 1 + i, span(b)] = result[i * tile : (i + 1) * tile]

    def sideways(b, side):
        peer = lax.rem(col + 1, cols) if side == 0 else lax.rem(col + cols - 1, cols)
        return pltpu.make_async_remote_copy(
            src_ref=edges.at[b, side], dst_ref=halo.at[b, side],
            send_sem=edge_send.at[b, side], recv_sem=edge_recv.at[b, side],
            device_id={"cols": peer}, device_id_type=MESH,
        )

    sends_side = (col < cols - 1, col > 0)
    takes_side = (col > 0, col < cols - 1)

    def window(ref, b, a):
        start = b * lines + a
        return ref[:, start : start + lines].reshape(halves * tile, channels)

    def place_band(ref, b, value):
        ref[:, 1 + b * lines : 1 + (b + 1) * lines] = value.reshape(halves, lines, strip, channels)

    def reduce_band(b):
        summed = jnp.zeros((halves * tile, channels), f32) + bd[...]
        for k in range(3):
            which = [2 * s + 2 - k for s in range(halves)]
            summed = summed + jnp.dot(stacked(lifted, which, b), wd[k], preferred_element_type=f32)
        reduced = summed.astype(bf16)
        place_band(middle, b, reduced)
        wide = reduced.astype(f32).reshape(halves, lines, strip, channels)
        edges[b, 0] = wide[:, :, strip - 1].astype(bf16)
        edges[b, 1] = wide[:, :, 0].astype(bf16)
        for side in range(2):
            @pl.when(sends_side[side])
            def _():
                sideways(b, side).start()

    def shift_band(b):
        for side in range(2):
            @pl.when(takes_side[side])
            def _():
                sideways(b, side).wait_recv()

            @pl.when(jnp.logical_not(takes_side[side]))
            def _():
                halo[b, side] = jnp.zeros((halves, lines, channels), bf16)

        size = halves * tile
        wide = window(middle, b, 1).astype(f32)
        place = lax.rem(lax.broadcasted_iota(jnp.int32, (size, channels), 0), strip)

        def spread(side):
            column = halo[b, side].astype(f32)
            column = jnp.broadcast_to(column[:, :, None, :], (halves, lines, strip, channels))
            return column.reshape(size, channels)

        lower = jnp.where(place == 0, spread(0), pltpu.roll(wide, 1, 0))
        upper = jnp.where(place == strip - 1, spread(1), pltpu.roll(wide, size - 1, 0))
        place_band(left_of, b, lower.astype(bf16))
        place_band(right_of, b, upper.astype(bf16))

    def convolve_band(b):
        summed = jnp.zeros((halves * tile, channels), f32) + bs[...]
        for k, shifted in ((1, middle), (0, left_of), (2, right_of)):
            for a in range(3):
                summed = summed + jnp.dot(
                    window(shifted, b, a), ws[3 * a + k], preferred_element_type=f32
                )
        result = (window(middle, b, 1).astype(f32) + jax.nn.silu(summed)).astype(bf16)
        spatial[b] = result.reshape(halves, owners, pixels, channels)

    def outward(c, peer, slot, source):
        return pltpu.make_async_remote_copy(
            src_ref=spatial.at[c, :, peer],
            dst_ref=held.at[c, source],
            send_sem=send_sem.at[c, slot],
            recv_sem=recv_sem.at[c, source],
            device_id={"tm": peer},
            device_id_type=MESH,
        )

    def homeward(c, peer, slot, source):
        return pltpu.make_async_remote_copy(
            src_ref=done.at[c, peer],
            dst_ref=y_ref.at[:, c, source],
            send_sem=back_sem.at[c, slot],
            recv_sem=home_sem.at[c, source],
            device_id={"tm": peer},
            device_id_type=MESH,
        )

    def scatter(c):
        def send(k, _):
            outward(c, lax.rem(me + k, owners), k, me).start()
            return 0

        lax.fori_loop(1, owners, send, 0)

    def attend(c):
        held[c, me] = spatial[c, :, me]

        def arrive(k, _):
            source = lax.rem(me + owners - k, owners)
            outward(c, lax.rem(me + k, owners), k, source).wait_recv()
            return 0

        lax.fori_loop(1, owners, arrive, 0)
        place = lax.broadcasted_iota(jnp.int32, (rows, rows), 0)
        other = lax.broadcasted_iota(jnp.int32, (rows, rows), 1)
        allowed = (lax.rem(place, pixels) == lax.rem(other, pixels)) & (other <= place)
        wide = held[c].reshape(rows, channels).astype(f32)
        scale = lax.rsqrt(jnp.mean(wide * wide, axis=-1, keepdims=True) + epsilon)
        normed = (wide * scale * gain[...]).astype(bf16)
        query = jnp.dot(normed, wq[...], preferred_element_type=f32).astype(bf16)
        key = jnp.dot(normed, wk[...], preferred_element_type=f32).astype(bf16)
        value = jnp.dot(normed, wv[...], preferred_element_type=f32).astype(bf16)
        scores = lax.dot_general(
            query, key, (((1,), (1,)), ((), ())), preferred_element_type=f32
        ) * channels ** (-0.5)
        scores = jnp.where(allowed, scores, -1e30)
        largest = jnp.max(scores, axis=-1, keepdims=True)
        probs = jnp.exp(scores - largest)
        probs = (probs / jnp.sum(probs, axis=-1, keepdims=True)).astype(bf16)
        context = jnp.dot(probs, value, preferred_element_type=f32).astype(bf16)
        mixed = jnp.dot(context, wo[...], preferred_element_type=f32)
        result = (wide + mixed).astype(bf16)
        done[c] = result.reshape(owners, halves, pixels, channels)

        def back(k, _):
            homeward(c, lax.rem(me + k, owners), k, me).start()
            return 0

        lax.fori_loop(1, owners, back, 0)
        y_ref[:, c, me] = done[c, me]

    for shifted in (left_of, middle, right_of):
        for line in (0, height + 1):
            shifted[:, line] = jnp.zeros((halves, strip, channels), bf16)
    loads[0].wait()
    send_on(0, 0)
    send_on(1, 0)
    loads[1].wait()
    for b in range(chunks):
        lift(2, frames - 2, b)
        send_on(2, b)
        if b + 1 < chunks:
            send_on(0, b + 1)
            send_on(1, b + 1)
    for load in loads[2:]:
        load.wait()
    for b in range(chunks + 1):
        if b < chunks:
            take(0, b)
            take(1, b)
            lift(0, 2, b)
            take(2, b)
            reduce_band(b)
            shift_band(b)
        if b >= 1:
            convolve_band(b - 1)
            scatter(b - 1)
    for c in range(chunks):
        attend(c)

    @pl.when(has_next)
    def _():
        for b in range(chunks):
            for i in range(3):
                onward(i, b).wait_send()

    for b in range(chunks):
        for side in range(2):
            @pl.when(sends_side[side])
            def _():
                sideways(b, side).wait_send()

    for c in range(chunks):
        def finish(k, _):
            peer, source = lax.rem(me + k, owners), lax.rem(me + owners - k, owners)
            outward(c, peer, k, me).wait_send()
            homeward(c, peer, k, me).wait_send()
            homeward(c, peer, k, source).wait_recv()
            return 0

        lax.fori_loop(1, owners, finish, 0)


def per_device(
    video, w_time, b_time, w_down, b_down, w_space, b_space, gain, w_query, w_key, w_value, w_out
):
    frames, height, strip, channels = video.shape
    halves, owners, area = frames // 2, lax.axis_size("tm"), height * strip
    owned = area // owners
    pixels = min(16, owned)
    chunks = owned // pixels
    vmem = pl.BlockSpec(memory_space=pltpu.VMEM)
    hbm = pl.BlockSpec(memory_space=pltpu.HBM)
    bf16 = jnp.bfloat16
    square = (channels, channels)
    shifted = pltpu.VMEM((halves, height + 2, strip, channels), bf16)
    flat = lambda v: v.reshape(1, channels)
    sems = pltpu.SemaphoreType.DMA
    result = pl.pallas_call(
        partial(block_kernel, (height, strip)),
        out_shape=jax.ShapeDtypeStruct((halves, chunks, owners, pixels, channels), bf16),
        in_specs=[hbm, hbm, vmem, hbm, vmem, hbm, vmem, vmem, hbm, hbm, hbm, hbm],
        out_specs=vmem,
        scratch_shapes=[
            pltpu.VMEM((3,) + square, bf16),
            pltpu.VMEM((3,) + square, bf16),
            pltpu.VMEM((9,) + square, bf16),
            pltpu.VMEM(square, bf16),
            pltpu.VMEM(square, bf16),
            pltpu.VMEM(square, bf16),
            pltpu.VMEM(square, bf16),
            pltpu.VMEM((frames + 2, area, channels), bf16),
            pltpu.VMEM((frames + 1, area, channels), bf16),
            shifted,
            shifted,
            shifted,
            pltpu.VMEM((chunks, 2, halves, height // chunks, channels), bf16),
            pltpu.VMEM((chunks, 2, halves, height // chunks, channels), bf16),
            pltpu.VMEM((chunks, halves, owners, pixels, channels), bf16),
            pltpu.VMEM((chunks, owners, halves, pixels, channels), bf16),
            pltpu.VMEM((chunks, owners, halves, pixels, channels), bf16),
            sems((8,)),
            sems((3, chunks)),
            sems((3, chunks)),
            sems((chunks, 2)),
            sems((chunks, 2)),
            sems((chunks, owners)),
            sems((chunks, owners)),
            sems((chunks, owners)),
            sems((chunks, owners)),
        ],
        compiler_params=pltpu.CompilerParams(
            collective_id=0, has_side_effects=True, vmem_limit_bytes=44 * 1024 * 1024
        ),
    )(
        video.reshape(frames, area, channels), w_time, flat(b_time), w_down, flat(b_down),
        w_space, flat(b_space), flat(gain), w_query, w_key, w_value, w_out,
    )
    return result.reshape(halves, height, strip, channels)


def solution(mesh):
    return jax.shard_map(
        per_device,
        mesh=mesh,
        in_specs=(P(("clips", "tm"), None, "cols", None),) + (P(),) * 11,
        out_specs=P(("clips", "tm"), None, "cols", None),
        check_vma=False,
    )
```

```python
from functools import partial

import jax
import jax.numpy as jnp
from jax import lax
from jax.experimental import pallas as pl
from jax.experimental.pallas import tpu as pltpu
from jax.sharding import PartitionSpec as P

epsilon = 1e-06
MESH = pl.DeviceIdType.MESH


def block_kernel(
    shape, video_hbm, wt_hbm, bt, wd_hbm, bd, ws_hbm, bs, gain, wq_hbm, wk_hbm, wv_hbm, wo_hbm, y_ref,
    wt, wd, ws, wq, wk, wv, wo, video, lifted, left_of, middle, right_of,
    edges, halo, spatial, held, done,
    load_sem, frame_send, frame_recv, edge_send, edge_recv, send_sem, recv_sem, back_sem, home_sem,
):
    height, strip = shape
    frames, area, channels = video_hbm.shape
    halves, chunks, owners, pixels, _ = y_ref.shape
    total = owners * halves
    rows = total * pixels
    me, col, cols = lax.axis_index("tm"), lax.axis_index("cols"), lax.axis_size("cols")
    f32, bf16 = jnp.float32, jnp.bfloat16
    tile = owners * pixels
    lines = tile // strip

    loads = [
        pltpu.make_async_copy(source, target, load_sem.at[i])
        for i, (source, target) in enumerate(
            (
                (video_hbm, video.at[pl.ds(2, frames)]), (wt_hbm, wt), (wd_hbm, wd), (ws_hbm, ws),
                (wq_hbm, wq), (wk_hbm, wk), (wv_hbm, wv), (wo_hbm, wo),
            )
        )
    ]
    for load in loads:
        load.start()

    barrier = pltpu.get_barrier_semaphore()

    def greet(k, _):
        peer = lax.rem(me + k, owners)
        pl.semaphore_signal(barrier, inc=1, device_id={"tm": peer}, device_id_type=MESH)
        return 0

    lax.fori_loop(1, owners, greet, 0)

    def greet_side(k, _):
        peer = lax.rem(col + k, cols)
        pl.semaphore_signal(barrier, inc=1, device_id={"cols": peer}, device_id_type=MESH)
        return 0

    lax.fori_loop(1, cols, greet_side, 0)
    pl.semaphore_wait(barrier, owners + cols - 2)

    has_next, has_before = me < owners - 1, me > 0

    def span(b):
        return pl.ds(b * tile, tile)

    def landing(i, b):
        return (video.at[1, span(b)], video.at[0, span(b)], lifted.at[0, span(b)])[i]

    def onward(i, b):
        source = (video.at[frames + 1, span(b)], video.at[frames, span(b)], lifted.at[frames, span(b)])[i]
        return pltpu.make_async_remote_copy(
            src_ref=source, dst_ref=landing(i, b),
            send_sem=frame_send.at[i, b], recv_sem=frame_recv.at[i, b],
            device_id={"tm": lax.rem(me + 1, owners)}, device_id_type=MESH,
        )

    def send_on(i, b):
        @pl.when(has_next)
        def _():
            onward(i, b).start()

    def take(i, b):
        @pl.when(has_before)
        def _():
            onward(i, b).wait_recv()

        @pl.when(jnp.logical_not(has_before))
        def _():
            landing(i, b)[...] = jnp.zeros((tile, channels), bf16)

    def stacked(ref, which, b):
        return jnp.concatenate([ref[f, span(b)] for f in which], 0)

    def lift(first, count, b):
        own = [f + 2 for f in range(first, first + count)]
        summed = jnp.dot(stacked(video, own, b), wt[0], preferred_element_type=f32)
        for k in (1, 2):
            summed = summed + jnp.dot(
                stacked(video, [f - k for f in own], b), wt[k], preferred_element_type=f32
            )
        summed = summed + bt[...]
        result = (stacked(video, own, b).astype(f32) + jax.nn.silu(summed)).astype(bf16)
        for i in range(count):
            lifted[first + 1 + i, span(b)] = result[i * tile : (i + 1) * tile]

    def sideways(b, side):
        peer = lax.rem(col + 1, cols) if side == 0 else lax.rem(col + cols - 1, cols)
        return pltpu.make_async_remote_copy(
            src_ref=edges.at[b, side], dst_ref=halo.at[b, side],
            send_sem=edge_send.at[b, side], recv_sem=edge_recv.at[b, side],
            device_id={"cols": peer}, device_id_type=MESH,
        )

    sends_side = (col < cols - 1, col > 0)
    takes_side = (col > 0, col < cols - 1)

    def window(ref, b, a):
        start = b * lines + a
        return ref[:, start : start + lines].reshape(halves * tile, channels)

    def place_band(ref, b, value):
        ref[:, 1 + b * lines : 1 + (b + 1) * lines] = value.reshape(halves, lines, strip, channels)

    def reduce_band(b):
        summed = jnp.zeros((halves * tile, channels), f32) + bd[...]
        for k in range(3):
            which = [2 * s + 2 - k for s in range(halves)]
            summed = summed + jnp.dot(stacked(lifted, which, b), wd[k], preferred_element_type=f32)
        reduced = summed.astype(bf16)
        place_band(middle, b, reduced)
        wide = reduced.astype(f32).reshape(halves, lines, strip, channels)
        edges[b, 0] = wide[:, :, strip - 1].astype(bf16)
        edges[b, 1] = wide[:, :, 0].astype(bf16)
        for side in range(2):
            @pl.when(sends_side[side])
            def _():
                sideways(b, side).start()

    def shift_band(b):
        for side in range(2):
            @pl.when(takes_side[side])
            def _():
                sideways(b, side).wait_recv()

            @pl.when(jnp.logical_not(takes_side[side]))
            def _():
                halo[b, side] = jnp.zeros((halves, lines, channels), bf16)

        size = halves * tile
        wide = window(middle, b, 1).astype(f32)
        place = lax.rem(lax.broadcasted_iota(jnp.int32, (size, channels), 0), strip)

        def spread(side):
            column = halo[b, side].astype(f32)
            column = jnp.broadcast_to(column[:, :, None, :], (halves, lines, strip, channels))
            return column.reshape(size, channels)

        lower = jnp.where(place == 0, spread(0), pltpu.roll(wide, 1, 0))
        upper = jnp.where(place == strip - 1, spread(1), pltpu.roll(wide, size - 1, 0))
        place_band(left_of, b, lower.astype(bf16))
        place_band(right_of, b, upper.astype(bf16))

    def convolve_band(b):
        summed = jnp.zeros((halves * tile, channels), f32) + bs[...]
        for k, shifted in ((1, middle), (0, left_of), (2, right_of)):
            for a in range(3):
                summed = summed + jnp.dot(
                    window(shifted, b, a), ws[3 * a + k], preferred_element_type=f32
                )
        result = (window(middle, b, 1).astype(f32) + jax.nn.silu(summed)).astype(bf16)
        spatial[b] = result.reshape(halves, owners, pixels, channels)

    def outward(c, peer, slot, source):
        return pltpu.make_async_remote_copy(
            src_ref=spatial.at[c, :, peer],
            dst_ref=held.at[c, source],
            send_sem=send_sem.at[c, slot],
            recv_sem=recv_sem.at[c, source],
            device_id={"tm": peer},
            device_id_type=MESH,
        )

    def homeward(c, peer, slot, source):
        return pltpu.make_async_remote_copy(
            src_ref=done.at[c, peer],
            dst_ref=y_ref.at[:, c, source],
            send_sem=back_sem.at[c, slot],
            recv_sem=home_sem.at[c, source],
            device_id={"tm": peer},
            device_id_type=MESH,
        )

    def scatter(c):
        def send(k, _):
            outward(c, lax.rem(me + k, owners), k, me).start()
            return 0

        lax.fori_loop(1, owners, send, 0)

    def attend(c):
        held[c, me] = spatial[c, :, me]

        def arrive(k, _):
            source = lax.rem(me + owners - k, owners)
            outward(c, lax.rem(me + k, owners), k, source).wait_recv()
            return 0

        lax.fori_loop(1, owners, arrive, 0)
        place = lax.broadcasted_iota(jnp.int32, (rows, rows), 0)
        other = lax.broadcasted_iota(jnp.int32, (rows, rows), 1)
        allowed = (lax.rem(place, pixels) == lax.rem(other, pixels)) & (other <= place)
        wide = held[c].reshape(rows, channels).astype(f32)
        scale = lax.rsqrt(jnp.mean(wide * wide, axis=-1, keepdims=True) + epsilon)
        normed = (wide * scale * gain[...]).astype(bf16)
        query = jnp.dot(normed, wq[...], preferred_element_type=f32).astype(bf16)
        key = jnp.dot(normed, wk[...], preferred_element_type=f32).astype(bf16)
        value = jnp.dot(normed, wv[...], preferred_element_type=f32).astype(bf16)
        scores = lax.dot_general(
            query, key, (((1,), (1,)), ((), ())), preferred_element_type=f32
        ) * channels ** (-0.5)
        scores = jnp.where(allowed, scores, -1e30)
        largest = jnp.max(scores, axis=-1, keepdims=True)
        probs = jnp.exp(scores - largest)
        probs = (probs / jnp.sum(probs, axis=-1, keepdims=True)).astype(bf16)
        context = jnp.dot(probs, value, preferred_element_type=f32).astype(bf16)
        mixed = jnp.dot(context, wo[...], preferred_element_type=f32)
        result = (wide + mixed).astype(bf16)
        done[c] = result.reshape(owners, halves, pixels, channels)

        def back(k, _):
            homeward(c, lax.rem(me + k, owners), k, me).start()
            return 0

        lax.fori_loop(1, owners, back, 0)
        y_ref[:, c, me] = done[c, me]

    for shifted in (left_of, middle, right_of):
        for line in (0, height + 1):
            shifted[:, line] = jnp.zeros((halves, strip, channels), bf16)
    loads[0].wait()
    send_on(0, 0)
    send_on(1, 0)
    loads[1].wait()
    for b in range(chunks):
        lift(2, frames - 2, b)
        send_on(2, b)
        if b + 1 < chunks:
            send_on(0, b + 1)
            send_on(1, b + 1)
    for load in loads[2:]:
        load.wait()
    for b in range(chunks + 1):
        if b < chunks:
            take(0, b)
            take(1, b)
            lift(0, 2, b)
            take(2, b)
            reduce_band(b)
            shift_band(b)
        if b >= 1:
            convolve_band(b - 1)
            scatter(b - 1)
    for c in range(chunks):
        attend(c)

    @pl.when(has_next)
    def _():
        for b in range(chunks):
            for i in range(3):
                onward(i, b).wait_send()

    for b in range(chunks):
        for side in range(2):
            @pl.when(sends_side[side])
            def _():
                sideways(b, side).wait_send()

    for c in range(chunks):
        def finish(k, _):
            peer, source = lax.rem(me + k, owners), lax.rem(me + owners - k, owners)
            outward(c, peer, k, me).wait_send()
            homeward(c, peer, k, me).wait_send()
            homeward(c, peer, k, source).wait_recv()
            return 0

        lax.fori_loop(1, owners, finish, 0)


def per_device(
    video, w_time, b_time, w_down, b_down, w_space, b_space, gain, w_query, w_key, w_value, w_out
):
    frames, height, strip, channels = video.shape
    halves, owners, area = frames // 2, lax.axis_size("tm"), height * strip
    owned = area // owners
    pixels = min(16, owned)
    chunks = owned // pixels
    vmem = pl.BlockSpec(memory_space=pltpu.VMEM)
    hbm = pl.BlockSpec(memory_space=pltpu.HBM)
    bf16 = jnp.bfloat16
    square = (channels, channels)
    shifted = pltpu.VMEM((halves, height + 2, strip, channels), bf16)
    flat = lambda v: v.reshape(1, channels)
    sems = pltpu.SemaphoreType.DMA
    result = pl.pallas_call(
        partial(block_kernel, (height, strip)),
        out_shape=jax.ShapeDtypeStruct((halves, chunks, owners, pixels, channels), bf16),
        in_specs=[hbm, hbm, vmem, hbm, vmem, hbm, vmem, vmem, hbm, hbm, hbm, hbm],
        out_specs=vmem,
        scratch_shapes=[
            pltpu.VMEM((3,) + square, bf16),
            pltpu.VMEM((3,) + square, bf16),
            pltpu.VMEM((9,) + square, bf16),
            pltpu.VMEM(square, bf16),
            pltpu.VMEM(square, bf16),
            pltpu.VMEM(square, bf16),
            pltpu.VMEM(square, bf16),
            pltpu.VMEM((frames + 2, area, channels), bf16),
            pltpu.VMEM((frames + 1, area, channels), bf16),
            shifted,
            shifted,
            shifted,
            pltpu.VMEM((chunks, 2, halves, height // chunks, channels), bf16),
            pltpu.VMEM((chunks, 2, halves, height // chunks, channels), bf16),
            pltpu.VMEM((chunks, halves, owners, pixels, channels), bf16),
            pltpu.VMEM((chunks, owners, halves, pixels, channels), bf16),
            pltpu.VMEM((chunks, owners, halves, pixels, channels), bf16),
            sems((8,)),
            sems((3, chunks)),
            sems((3, chunks)),
            sems((chunks, 2)),
            sems((chunks, 2)),
            sems((chunks, owners)),
            sems((chunks, owners)),
            sems((chunks, owners)),
            sems((chunks, owners)),
        ],
        compiler_params=pltpu.CompilerParams(
            collective_id=0, has_side_effects=True, vmem_limit_bytes=57 * 1024 * 1024
        ),
    )(
        video.reshape(frames, area, channels), w_time, flat(b_time), w_down, flat(b_down),
        w_space, flat(b_space), flat(gain), w_query, w_key, w_value, w_out,
    )
    return result.reshape(halves, height, strip, channels)


def solution(mesh):
    return jax.shard_map(
        per_device,
        mesh=mesh,
        in_specs=(P(("clips", "tm"), None, "cols", None),) + (P(),) * 11,
        out_specs=P(("clips", "tm"), None, "cols", None),
        check_vma=False,
    )
```

```python
from functools import partial

import jax
import jax.numpy as jnp
from jax import lax
from jax.experimental import pallas as pl
from jax.experimental.pallas import tpu as pltpu
from jax.sharding import PartitionSpec as P

epsilon = 1e-06
MESH = pl.DeviceIdType.MESH


def block_kernel(
    shape, video_hbm, wt_hbm, bt, wd_hbm, bd, ws_hbm, bs, gain, wq_hbm, wk_hbm, wv_hbm, wo_hbm, y_ref,
    wt, wd, ws, wq, wk, wv, wo, video, lifted, left_of, middle, right_of,
    edges, halo, spatial, held, done,
    load_sem, frame_send, frame_recv, edge_send, edge_recv, send_sem, recv_sem, back_sem, home_sem,
):
    height, strip = shape
    frames, area, channels = video_hbm.shape
    halves, chunks, owners, pixels, _ = y_ref.shape
    total = owners * halves
    rows = total * pixels
    me, col, cols = lax.axis_index("tm"), lax.axis_index("cols"), lax.axis_size("cols")
    f32, bf16 = jnp.float32, jnp.bfloat16
    tile = owners * pixels
    lines = tile // strip

    loads = [
        pltpu.make_async_copy(source, target, load_sem.at[i])
        for i, (source, target) in enumerate(
            (
                (video_hbm, video.at[pl.ds(2, frames)]), (wt_hbm, wt), (wd_hbm, wd), (ws_hbm, ws),
                (wq_hbm, wq), (wk_hbm, wk), (wv_hbm, wv), (wo_hbm, wo),
            )
        )
    ]
    for load in loads:
        load.start()

    barrier = pltpu.get_barrier_semaphore()

    def greet(k, _):
        peer = lax.rem(me + k, owners)
        pl.semaphore_signal(barrier, inc=1, device_id={"tm": peer}, device_id_type=MESH)
        return 0

    lax.fori_loop(1, owners, greet, 0)

    def greet_side(k, _):
        peer = lax.rem(col + k, cols)
        pl.semaphore_signal(barrier, inc=1, device_id={"cols": peer}, device_id_type=MESH)
        return 0

    lax.fori_loop(1, cols, greet_side, 0)
    pl.semaphore_wait(barrier, owners + cols - 2)

    has_next, has_before = me < owners - 1, me > 0

    def span(b):
        return pl.ds(b * tile, tile)

    def landing(i, b):
        return (video.at[1, span(b)], video.at[0, span(b)], lifted.at[0, span(b)])[i]

    def onward(i, b):
        source = (video.at[frames + 1, span(b)], video.at[frames, span(b)], lifted.at[frames, span(b)])[i]
        return pltpu.make_async_remote_copy(
            src_ref=source, dst_ref=landing(i, b),
            send_sem=frame_send.at[i, b], recv_sem=frame_recv.at[i, b],
            device_id={"tm": lax.rem(me + 1, owners)}, device_id_type=MESH,
        )

    def send_on(i, b):
        @pl.when(has_next)
        def _():
            onward(i, b).start()

    def take(i, b):
        @pl.when(has_before)
        def _():
            onward(i, b).wait_recv()

        @pl.when(jnp.logical_not(has_before))
        def _():
            landing(i, b)[...] = jnp.zeros((tile, channels), bf16)

    def stacked(ref, which, b):
        return jnp.concatenate([ref[f, span(b)] for f in which], 0)

    def lift(first, count, b):
        own = [f + 2 for f in range(first, first + count)]
        summed = jnp.dot(stacked(video, own, b), wt[0], preferred_element_type=f32)
        for k in (1, 2):
            summed = summed + jnp.dot(
                stacked(video, [f - k for f in own], b), wt[k], preferred_element_type=f32
            )
        summed = summed + bt[...]
        result = (stacked(video, own, b).astype(f32) + jax.nn.silu(summed)).astype(bf16)
        for i in range(count):
            lifted[first + 1 + i, span(b)] = result[i * tile : (i + 1) * tile]

    def sideways(b, side):
        peer = lax.rem(col + 1, cols) if side == 0 else lax.rem(col + cols - 1, cols)
        return pltpu.make_async_remote_copy(
            src_ref=edges.at[b, side], dst_ref=halo.at[b, side],
            send_sem=edge_send.at[b, side], recv_sem=edge_recv.at[b, side],
            device_id={"cols": peer}, device_id_type=MESH,
        )

    sends_side = (col < cols - 1, col > 0)
    takes_side = (col > 0, col < cols - 1)

    def window(ref, b, a):
        start = b * lines + a
        return ref[:, start : start + lines].reshape(halves * tile, channels)

    def place_band(ref, b, value):
        ref[:, 1 + b * lines : 1 + (b + 1) * lines] = value.reshape(halves, lines, strip, channels)

    def reduce_band(b):
        summed = jnp.zeros((halves * tile, channels), f32) + bd[...]
        for k in range(3):
            which = [2 * s + 2 - k for s in range(halves)]
            summed = summed + jnp.dot(stacked(lifted, which, b), wd[k], preferred_element_type=f32)
        reduced = summed.astype(bf16)
        place_band(middle, b, reduced)
        wide = reduced.astype(f32).reshape(halves, lines, strip, channels)
        edges[b, 0] = wide[:, :, strip - 1].astype(bf16)
        edges[b, 1] = wide[:, :, 0].astype(bf16)
        for side in range(2):
            @pl.when(sends_side[side])
            def _():
                sideways(b, side).start()

    def shift_band(b):
        for side in range(2):
            @pl.when(takes_side[side])
            def _():
                sideways(b, side).wait_recv()

            @pl.when(jnp.logical_not(takes_side[side]))
            def _():
                halo[b, side] = jnp.zeros((halves, lines, channels), bf16)

        size = halves * tile
        wide = window(middle, b, 1).astype(f32)
        place = lax.rem(lax.broadcasted_iota(jnp.int32, (size, channels), 0), strip)

        def spread(side):
            column = halo[b, side].astype(f32)
            column = jnp.broadcast_to(column[:, :, None, :], (halves, lines, strip, channels))
            return column.reshape(size, channels)

        lower = jnp.where(place == 0, spread(0), pltpu.roll(wide, 1, 0))
        upper = jnp.where(place == strip - 1, spread(1), pltpu.roll(wide, size - 1, 0))
        place_band(left_of, b, lower.astype(bf16))
        place_band(right_of, b, upper.astype(bf16))

    def convolve_band(b):
        summed = jnp.zeros((halves * tile, channels), f32) + bs[...]
        for k, shifted in ((1, middle), (0, left_of), (2, right_of)):
            for a in range(3):
                summed = summed + jnp.dot(
                    window(shifted, b, a), ws[3 * a + k], preferred_element_type=f32
                )
        result = (window(middle, b, 1).astype(f32) + jax.nn.silu(summed)).astype(bf16)
        spatial[b] = result.reshape(halves, owners, pixels, channels)

    def outward(c, peer, slot, source):
        return pltpu.make_async_remote_copy(
            src_ref=spatial.at[c, :, peer],
            dst_ref=held.at[c, source],
            send_sem=send_sem.at[c, slot],
            recv_sem=recv_sem.at[c, source],
            device_id={"tm": peer},
            device_id_type=MESH,
        )

    def homeward(c, peer, slot, source):
        return pltpu.make_async_remote_copy(
            src_ref=done.at[c, peer],
            dst_ref=y_ref.at[:, c, source],
            send_sem=back_sem.at[c, slot],
            recv_sem=home_sem.at[c, source],
            device_id={"tm": peer},
            device_id_type=MESH,
        )

    def scatter(c):
        def send(k, _):
            outward(c, lax.rem(me + k, owners), k, me).start()
            return 0

        lax.fori_loop(1, owners, send, 0)

    def attend(c):
        held[c, me] = spatial[c, :, me]

        def arrive(k, _):
            source = lax.rem(me + owners - k, owners)
            outward(c, lax.rem(me + k, owners), k, source).wait_recv()
            return 0

        lax.fori_loop(1, owners, arrive, 0)
        place = lax.broadcasted_iota(jnp.int32, (rows, rows), 0)
        other = lax.broadcasted_iota(jnp.int32, (rows, rows), 1)
        allowed = (lax.rem(place, pixels) == lax.rem(other, pixels)) & (other <= place)
        wide = held[c].reshape(rows, channels).astype(f32)
        scale = lax.rsqrt(jnp.mean(wide * wide, axis=-1, keepdims=True) + epsilon)
        normed = (wide * scale * gain[...]).astype(bf16)
        query = jnp.dot(normed, wq[...], preferred_element_type=f32).astype(bf16)
        key = jnp.dot(normed, wk[...], preferred_element_type=f32).astype(bf16)
        value = jnp.dot(normed, wv[...], preferred_element_type=f32).astype(bf16)
        scores = lax.dot_general(
            query, key, (((1,), (1,)), ((), ())), preferred_element_type=f32
        ) * channels ** (-0.5)
        scores = jnp.where(allowed, scores, -1e30)
        largest = jnp.max(scores, axis=-1, keepdims=True)
        probs = jnp.exp(scores - largest)
        probs = (probs / jnp.sum(probs, axis=-1, keepdims=True)).astype(bf16)
        context = jnp.dot(probs, value, preferred_element_type=f32).astype(bf16)
        mixed = jnp.dot(context, wo[...], preferred_element_type=f32)
        result = (wide + mixed).astype(bf16)
        done[c] = result.reshape(owners, halves, pixels, channels)

        def back(k, _):
            homeward(c, lax.rem(me + k, owners), k, me).start()
            return 0

        lax.fori_loop(1, owners, back, 0)
        y_ref[:, c, me] = done[c, me]

    for shifted in (left_of, middle, right_of):
        for line in (0, height + 1):
            shifted[:, line] = jnp.zeros((halves, strip, channels), bf16)
    loads[0].wait()
    send_on(0, 0)
    send_on(1, 0)
    loads[1].wait()
    for b in range(chunks):
        lift(2, frames - 2, b)
        send_on(2, b)
        if b + 1 < chunks:
            send_on(0, b + 1)
            send_on(1, b + 1)
    for load in loads[2:]:
        load.wait()
    for b in range(chunks + 1):
        if b < chunks:
            take(0, b)
            take(1, b)
            lift(0, 2, b)
            take(2, b)
            reduce_band(b)
            shift_band(b)
        if b >= 1:
            if b == chunks and chunks > 1:
                attend(0)
            convolve_band(b - 1)
            scatter(b - 1)
    for c in range(min(1, chunks - 1), chunks):
        attend(c)

    @pl.when(has_next)
    def _():
        for b in range(chunks):
            for i in range(3):
                onward(i, b).wait_send()

    for b in range(chunks):
        for side in range(2):
            @pl.when(sends_side[side])
            def _():
                sideways(b, side).wait_send()

    for c in range(chunks):
        def finish(k, _):
            peer, source = lax.rem(me + k, owners), lax.rem(me + owners - k, owners)
            outward(c, peer, k, me).wait_send()
            homeward(c, peer, k, me).wait_send()
            homeward(c, peer, k, source).wait_recv()
            return 0

        lax.fori_loop(1, owners, finish, 0)


def per_device(
    video, w_time, b_time, w_down, b_down, w_space, b_space, gain, w_query, w_key, w_value, w_out
):
    frames, height, strip, channels = video.shape
    halves, owners, area = frames // 2, lax.axis_size("tm"), height * strip
    owned = area // owners
    pixels = min(16, owned)
    chunks = owned // pixels
    vmem = pl.BlockSpec(memory_space=pltpu.VMEM)
    hbm = pl.BlockSpec(memory_space=pltpu.HBM)
    bf16 = jnp.bfloat16
    square = (channels, channels)
    shifted = pltpu.VMEM((halves, height + 2, strip, channels), bf16)
    flat = lambda v: v.reshape(1, channels)
    sems = pltpu.SemaphoreType.DMA
    result = pl.pallas_call(
        partial(block_kernel, (height, strip)),
        out_shape=jax.ShapeDtypeStruct((halves, chunks, owners, pixels, channels), bf16),
        in_specs=[hbm, hbm, vmem, hbm, vmem, hbm, vmem, vmem, hbm, hbm, hbm, hbm],
        out_specs=vmem,
        scratch_shapes=[
            pltpu.VMEM((3,) + square, bf16),
            pltpu.VMEM((3,) + square, bf16),
            pltpu.VMEM((9,) + square, bf16),
            pltpu.VMEM(square, bf16),
            pltpu.VMEM(square, bf16),
            pltpu.VMEM(square, bf16),
            pltpu.VMEM(square, bf16),
            pltpu.VMEM((frames + 2, area, channels), bf16),
            pltpu.VMEM((frames + 1, area, channels), bf16),
            shifted,
            shifted,
            shifted,
            pltpu.VMEM((chunks, 2, halves, height // chunks, channels), bf16),
            pltpu.VMEM((chunks, 2, halves, height // chunks, channels), bf16),
            pltpu.VMEM((chunks, halves, owners, pixels, channels), bf16),
            pltpu.VMEM((chunks, owners, halves, pixels, channels), bf16),
            pltpu.VMEM((chunks, owners, halves, pixels, channels), bf16),
            sems((8,)),
            sems((3, chunks)),
            sems((3, chunks)),
            sems((chunks, 2)),
            sems((chunks, 2)),
            sems((chunks, owners)),
            sems((chunks, owners)),
            sems((chunks, owners)),
            sems((chunks, owners)),
        ],
        compiler_params=pltpu.CompilerParams(
            collective_id=0, has_side_effects=True, vmem_limit_bytes=57 * 1024 * 1024
        ),
    )(
        video.reshape(frames, area, channels), w_time, flat(b_time), w_down, flat(b_down),
        w_space, flat(b_space), flat(gain), w_query, w_key, w_value, w_out,
    )
    return result.reshape(halves, height, strip, channels)


def solution(mesh):
    return jax.shard_map(
        per_device,
        mesh=mesh,
        in_specs=(P(("clips", "tm"), None, "cols", None),) + (P(),) * 11,
        out_specs=P(("clips", "tm"), None, "cols", None),
        check_vma=False,
    )
```
